1024 devices in a mesh: row: 64 (over x, z), col: 16 (over y, core).
Axes of the slice: x: 8, y: 8, z: 8, core: 2. Of those that a mesh axis runs over, the one named last changes fastest.
Arguments:
- kernel: bfloat16 [2048, 256, 256], P(('row', 'col')), may hold values from -0.046875 to 0.046875
- intersection: bfloat16 [32, 256, 128], replicated, may hold values from -0.375 to 0.375
- momentum: int32 [256], replicated, may hold values from 0 to 31
- owner_pick: int32 [16384], P(('row', 'col')), may hold values from 0 to 1
- live_count: int32 [1024], P(('row', 'col')), may hold values from 1 to 16, as said below
- pair_slot: int32 [16384, 4], P(('row', 'col')), may hold values from 0 to 15
- denominators: float32 [32768], P(('row', 'col')), may hold values from 0.5 to 6
- shifts: float32 [256], replicated, may hold values from 1 to 3
- vectors: bfloat16 [32768, 256], P(('row', 'col')), may hold values from -6 to 6
Outputs:
- new_vectors: float32 [32768, 256], P(('row', 'col'))
- residual: float32 [32768, 256], P(('row', 'col'))
The draws below stay inside these ranges and needn't reach their ends.
Inputs may be any that keep to these rules, and one draw needn't show every extreme that they name: `live_count`: at most 16 incoming kernel blocks are live for a tile, and some tile has all 16 in every draw.
All inputs are finite; a program needn't handle non-finite values.
Results may differ from the reference program's by a relative error of at most 0.0037.
Values may be sent and summed in bfloat16 or wider, within the bound.
A program may use at most 32 MiB of HBM per device.

```python
import jax
import jax.numpy as jnp
from jax import lax

CB = 256
FB = 128
NVEC = 256
NQ = 32
KB_DEV = 2
ROWS_DEV = 32
M = 32768
FR = 16
FC = 4
NKB = 2048
NFINE = 256
N_ROW = 64
N_COL = 16
DEVICES = 1024


def draw_live_count(key, part):
    first_key, second_key = jax.random.split(key)
    counts = jax.random.randint(first_key, (DEVICES,), 1, N_COL + 1, dtype=jnp.int32)
    fullest = jax.random.randint(second_key, (), 0, DEVICES, dtype=jnp.int32)
    positions = jnp.arange(DEVICES, dtype=jnp.int32)
    return jnp.where(positions == fullest, N_COL, counts).astype(jnp.int32)


def plant(entries, rng, low, high):
    longest = entries.shape.index(max(entries.shape))
    spots = []
    for shift in (0, 1):
        where = [jax.random.randint(jax.random.fold_in(rng, axis), (), 0, length) for axis, length in enumerate(entries.shape)]
        where[longest] = (where[longest] + shift) % entries.shape[longest]
        spots.append(tuple(where))
    return entries.at[spots[0]].set(low).at[spots[1]].set(high)


def level_of(stream_key, shape, shards, low, high):
    level, own = 1.0, jax.random.fold_in(stream_key, 6)
    for position, blocks in shards:
        draws = jnp.exp(jax.random.uniform(jax.random.fold_in(own, position), (blocks,), jnp.float32, low / len(shards), high / len(shards)))
        level = level * jnp.repeat(draws, shape[position] // blocks).reshape([-1 if axis == position else 1 for axis in range(len(shape))])
    return level


def noise(rng, dims, spread, most, cuts=(), held_as=jnp.bfloat16):
    gain = level_of(rng, dims, cuts, -0.22, 0.18) if cuts else 1.0
    entries = jax.random.normal(rng, dims, jnp.float32) * spread * gain
    return jnp.minimum(jnp.maximum(entries, -most), most).astype(held_as)


def setup_inputs(seed: int = 0) -> dict:
    arg_keys = jax.random.split(jax.random.key(seed), 10)
    return {
        "kernel": noise(arg_keys[0], (NKB, CB, CB), (M // 2) ** -0.5, 0.046875, ((0, 1024),)),
        "intersection": noise(arg_keys[1], (NQ, CB, FB), CB ** -0.5, 0.375),
        "momentum": plant(jax.random.randint(arg_keys[2], (NFINE,), 0, NQ), jax.random.fold_in(arg_keys[2], 1), 0, NQ - 1).astype(jnp.int32),
        "owner_pick": plant(jax.random.randint(arg_keys[3], (DEVICES * N_COL,), 0, KB_DEV), jax.random.fold_in(arg_keys[3], 1), 0, KB_DEV - 1).astype(jnp.int32),
        "live_count": draw_live_count(jax.random.fold_in(arg_keys[9], 71), 0),
        "pair_slot": plant(jax.random.randint(arg_keys[5], (DEVICES * FR, FC), 0, N_COL), jax.random.fold_in(arg_keys[5], 1), 0, N_COL - 1).astype(jnp.int32),
        "denominators": jnp.clip(0.5 + 5.5 * jax.random.uniform(arg_keys[6], (M,), jnp.float32) ** level_of(arg_keys[6], (M,), ((0, 1024),), -0.2, 0.2), 0.5, 6.0),
        "shifts": jnp.clip(jax.random.uniform(arg_keys[7], (NVEC,), jnp.float32, 1.0, 3.0), 1.0, 3.0),
        "vectors": noise(arg_keys[8], (M, NVEC), 1.0, 6.0, ((0, 1024),)),
    }


def build_tile(tile_index, kernel, intersection, momentum, owner_pick, live_count, pair_slot):
    row_pos = tile_index // N_COL
    col_pos = tile_index % N_COL
    slot_grid = lax.dynamic_slice_in_dim(pair_slot, (tile_index * FR).astype(jnp.int32), FR, 0)
    count_live = live_count[tile_index]
    sources = row_pos * N_COL + slot_grid
    block_index = sources * KB_DEV + owner_pick[sources * N_COL + col_pos]
    row_class = lax.dynamic_slice_in_dim(momentum, (col_pos * FR).astype(jnp.int32), FR, 0)
    col_class = lax.dynamic_slice_in_dim(momentum, (row_pos * FC).astype(jnp.int32), FC, 0)
    row_basis = intersection[row_class].astype(jnp.float32)
    col_basis = intersection[col_class].astype(jnp.float32)

    def one_column(column):
        chosen = kernel[block_index[:, column]].astype(jnp.float32)
        half_product = jnp.einsum("kxy,yf->kxf", chosen, col_basis[column]).astype(jnp.bfloat16)
        half_product = lax.optimization_barrier(half_product).astype(jnp.float32)
        fine_block = jnp.einsum("kxa,kxf->kaf", row_basis, half_product)
        alive = slot_grid[:, column] < count_live
        return jnp.where(alive[:, None, None], fine_block, jnp.zeros_like(fine_block)).astype(jnp.bfloat16)

    fine_blocks = lax.map(one_column, jnp.arange(FC, dtype=jnp.int32))
    return fine_blocks.transpose(1, 2, 0, 3).reshape(FR * FB, FC * FB)


def multiply(tiles, vectors):
    blocks = tiles.reshape(N_ROW, N_COL, FR * FB, FC * FB)
    grouped = vectors.reshape(N_ROW, FC * FB, NVEC)

    def one_group(col_pos):
        def add_row(total, row_pos):
            tile_now = blocks[row_pos, col_pos]
            return total + jnp.dot(tile_now, grouped[row_pos], preferred_element_type=jnp.float32), None

        total, unused = lax.scan(add_row, jnp.zeros((FR * FB, NVEC), jnp.float32), jnp.arange(N_ROW, dtype=jnp.int32))
        return total

    columns = lax.map(one_group, jnp.arange(N_COL, dtype=jnp.int32))
    return columns.reshape(N_COL, N_ROW, ROWS_DEV, NVEC).transpose(1, 0, 2, 3).reshape(M, NVEC)


def reference(kernel, intersection, momentum, owner_pick, live_count, pair_slot, denominators, shifts, vectors):
    def build_one(tile_index):
        return build_tile(tile_index, kernel, intersection, momentum, owner_pick, live_count, pair_slot)

    tiles = lax.map(build_one, jnp.arange(DEVICES, dtype=jnp.int32))
    divisor = jnp.maximum(jnp.abs(denominators[:, None] - shifts[None, :]), 1.0)
    start_vectors = vectors.astype(jnp.float32)
    first_resid = multiply(tiles, vectors) - shifts[None, :] * start_vectors
    next_vectors = (start_vectors - first_resid / divisor).astype(jnp.bfloat16)
    next_float = next_vectors.astype(jnp.float32)
    second_resid = multiply(tiles, next_vectors) - shifts[None, :] * next_float
    return next_float - second_resid / divisor, second_resid
```

```python
import functools

import jax
import jax.numpy as jnp
from jax import lax
from jax.experimental import pallas as pl
from jax.experimental.pallas import tpu as pltpu
from jax.sharding import PartitionSpec as P

F32 = jnp.float32
BF16 = jnp.bfloat16


def send(src, dst, send_sem, recv_sem, row, col):
    return pltpu.make_async_remote_copy(
        src_ref=src,
        dst_ref=dst,
        send_sem=send_sem,
        recv_sem=recv_sem,
        device_id={"row": row, "col": col},
        device_id_type=pl.DeviceIdType.MESH,
    )


def body(
    nx, nz, ny, fb,
    mom, picks, live, slots, inter_hbm, kern_hbm, den, shifts, vec,
    prod_out, next_out,
    inter, blk, half, basis, tile, held, nextv, pk, pk_own,
    part0, part1, rx0, rx1, ry0, ry1, sum0, sum1, acc0, acc1,
    loc, pk_s, pk_r, ag_s, ag_r, fw_s, fw_r, ring_s, ring_r, sib_s, sib_r, s1_s, s1_r, s2_s, s2_r,
):
    nc = 2 * ny
    pr = vec.shape[0]
    nv = vec.shape[1]
    hv = nv // 2
    fc = nc * pr // fb
    chunk = nz * pr
    nblk = chunk // fb
    hop = ny // 2

    row = lax.axis_index("row")
    c = lax.axis_index("col")
    x, z = row // nz, row % nz
    y, core = c // 2, c % 2
    other = y * 2 + (1 - core)

    copy_kern = pltpu.make_async_copy(kern_hbm, blk.at[c], loc.at[0])
    copy_inter = pltpu.make_async_copy(inter_hbm, inter, loc.at[1])
    copy_kern.start()
    copy_inter.start()

    lane = lax.broadcasted_iota(jnp.int32, (8, 128), 1)
    mine = jnp.zeros((8, 128), jnp.int32)
    for j in range(nc):
        mine = jnp.where(lane == j, picks[j], mine)
    pk_own[...] = mine
    pk[c] = mine

    barrier = pltpu.get_barrier_semaphore()
    for d in range(1, nc):
        pl.semaphore_signal(barrier, inc=1, device_id={"row": row, "col": (c + d) % nc}, device_id_type=pl.DeviceIdType.MESH)
    for d in range(1, nx):
        pl.semaphore_signal(barrier, inc=1, device_id={"row": ((x + d) % nx) * nz + z, "col": c}, device_id_type=pl.DeviceIdType.MESH)
    for d in range(1, nz):
        pl.semaphore_signal(barrier, inc=1, device_id={"row": x * nz + (z + d) % nz, "col": c}, device_id_type=pl.DeviceIdType.MESH)
    pl.semaphore_wait(barrier, nc - 1 + nx - 1 + nz - 1)

    pending = []

    pk_copies = []
    for d in range(1, nc):
        cp = send(pk_own, pk.at[c], pk_s.at[d], pk_r.at[d], row, (c + d) % nc)
        cp.start()
        pk_copies.append(cp)
    pending += pk_copies

    def order(n):
        return [n // 2 + ((i + 1) // 2) * (1 - 2 * (i % 2)) for i in range(n - 1)]

    def gather_start(p, src):
        copies = {}
        for d in order(ny):
            copies[d] = send(src, held.at[p, pl.ds(c * pr, pr)], ag_s.at[p, d], ag_r.at[p, d], row, ((y + d) % ny) * 2 + core)
            copies[d].start()
        copies[0] = send(src, held.at[p, pl.ds(c * pr, pr)], ag_s.at[p, 0], ag_r.at[p, 0], row, other)
        copies[0].start()
        held[p, pl.ds(c * pr, pr), :] = src[...]
        return copies

    def gather_relay(p, copies):
        for d in sorted(range(1, ny), key=lambda d: min(d, ny - d)):
            copies[d].wait_recv()
            rows = pl.ds((((y - d) % ny) * 2 + core) * pr, pr)
            cp = send(held.at[p, rows], held.at[p, rows], fw_s.at[p, d], fw_r.at[p, d], row, other)
            cp.start()
            copies[ny + d] = cp

    def gather_end(p, copies):
        copies[0].wait_recv()
        for d in range(1, ny):
            copies[ny + d].wait_recv()

    got0 = gather_start(0, vec)

    length = {(0, 0): hop, (0, 1): hop - 1, (1, 0): hop - 1, (1, 1): hop}
    lanes = [(0, 0), (1, 1), (0, 1), (1, 0)]
    step_to = [((y + 1) % ny) * 2 + core, ((y + ny - 1) % ny) * 2 + core]

    def source(way, t):
        return ((y - t) % ny if way == 0 else (y + t) % ny) * 2 + core

    ring = {}
    for way, k in lanes:
        if length[way, k] >= 1:
            cp = send(kern_hbm.at[k], blk.at[c, k], ring_s.at[way, 0, k], ring_r.at[way, 0, k], row, step_to[way])
            cp.start()
            ring[way, 1, k] = cp
    sib = {}
    for k in range(2):
        cp = send(kern_hbm.at[k], blk.at[c, k], sib_s.at[0, 0, k], sib_r.at[0, 0, k], row, other)
        cp.start()
        sib[0, 0, k] = cp

    copy_kern.wait()
    copy_inter.wait()
    for b in range(fc):
        basis[:, b * fb:(b + 1) * fb] = inter[mom[row * fc + b]]
    half[nc] = jnp.zeros(half.shape[1:], BF16)
    for cp in pk_copies:
        cp.wait_recv()

    wide = fc * fb
    cut = min(wide, 2 * fb)

    def half_of(src):
        flag = jnp.sum(jnp.where(lax.broadcasted_iota(jnp.int32, (1, 128), 1) == c, pk[src][0:1, :], 0).astype(F32), axis=1, keepdims=True)
        for j in range(wide // cut):
            cols = slice(j * cut, (j + 1) * cut)
            second = jnp.broadcast_to(flag, (blk.shape[2], cut)) > 0.5
            h0 = jnp.dot(blk[src, 0], basis[:, cols], preferred_element_type=F32)
            h1 = jnp.dot(blk[src, 1], basis[:, cols], preferred_element_type=F32)
            half[src, :, cols] = jnp.where(second, h1, h0).astype(BF16)

    def halves(t):
        ways = [0] if t == 0 else [0, 1]
        for way in ways:
            for k in range(2):
                if (way, t, k) in sib:
                    sib[way, t, k].wait_recv()
        if t == 0 or t == hop:
            spot = y if t == 0 else (y + hop) % ny

            def one(j, carry):
                half_of(spot * 2 + j)
                return carry

            lax.fori_loop(0, 2, one, 0)
        else:

            def one(j, carry):
                half_of(((y + ny + (1 - 2 * (j // 2)) * t) % ny) * 2 + j % 2)
                return carry

            lax.fori_loop(0, 4, one, 0)

    for t in range(1, hop + 1):
        for way, k in lanes:
            if t > length[way, k]:
                continue
            ring[way, t, k].wait_recv()
            src = source(way, t)
            if t < length[way, k]:
                cp = send(blk.at[src, k], blk.at[src, k], ring_s.at[way, t, k], ring_r.at[way, t, k], row, step_to[way])
                cp.start()
                ring[way, t + 1, k] = cp
            cp = send(blk.at[src, k], blk.at[src, k], sib_s.at[way, t, k], sib_r.at[way, t, k], row, other)
            cp.start()
            sib[way, t, k] = cp
        if t == 1:
            gather_relay(0, got0)
        halves(t - 1)
    halves(hop)
    pending += list(ring.values()) + list(sib.values()) + list(got0.values())
    gather_end(0, got0)

    def offset(i, n):
        return n // 2 + ((i + 1) // 2) * (1 - 2 * (i % 2))

    def reduce_rows(p):
        v = held[p]

        def rows_for(x2):
            for q in range(nblk):
                a = x2 * nblk + q
                rows = pl.ds(pl.multiple_of(a * fb, fb), fb)
                if p == 0:
                    parts = []
                    for b in range(fc):
                        slot = slots[a, b]
                        slot = jnp.where(slot < live[0], slot, nc)
                        parts.append(half[slot, :, b * fb:(b + 1) * fb])
                    picked = jnp.concatenate(parts, axis=1)
                    u = inter[mom[c * (nx * nblk) + a]]
                    fine = lax.dot_general(u, picked, (((0,), (0,)), ((), ())), preferred_element_type=F32)
                    tile[rows, :] = fine.astype(BF16)
                got = jnp.dot(tile[rows, :], v, preferred_element_type=F32).astype(BF16)
                part0[p, rows, :] = got[:, :hv]
                for j in range(fb // pr):
                    z2 = q * (fb // pr) + j
                    part1[p, z2, pl.ds(pl.multiple_of(x2 * pr, pr), pr), :] = got[j * pr:(j + 1) * pr, hv:]

        def x_copy(i):
            d = offset(i, nx)
            x2 = (x + d) % nx
            return send(part0.at[p, pl.ds(pl.multiple_of(x2 * chunk, chunk), chunk)], rx0.at[p, d], s1_s.at[p, 0, d], s1_r.at[p, 0, d], x2 * nz + z, c)

        def step(i, carry):
            rows_for((x + offset(i, nx)) % nx)
            x_copy(i).start()
            return carry

        if nx > 1:
            lax.fori_loop(0, nx - 1, step, 0)
        rows_for(x)

        def z_copy(d):
            z2 = (z + d) % nz
            return send(part1.at[p, z2], rx1.at[p, d], s1_s.at[p, 1, d], s1_r.at[p, 1, d], x * nz + z2, c)

        z_copies = {d: z_copy(d) for d in order(nz)}
        for d in order(nz):
            z_copies[d].start()
        x_copies = {offset(i, nx): x_copy(i) for i in range(nx - 1)}

        acc0[...] = part0[p, pl.ds(pl.multiple_of(x * chunk, chunk), chunk), :].astype(F32)
        acc1[...] = part1[p, z].astype(F32)
        for d in order(nx):
            x_copies[d].wait_recv()
            acc0[...] += rx0[p, d].astype(F32)
        sum0[p] = acc0[...].astype(BF16)
        last0 = {}
        for d in order(nz):
            z2 = (z + d) % nz
            last0[d] = send(sum0.at[p, pl.ds(pl.multiple_of(z2 * pr, pr), pr)], ry0.at[p, d], s2_s.at[p, 0, d], s2_r.at[p, 0, d], x * nz + z2, c)
            last0[d].start()
        for d in order(nz):
            z_copies[d].wait_recv()
            acc1[...] += rx1[p, d].astype(F32)
        sum1[p] = acc1[...].astype(BF16)
        last1 = {}
        for d in order(nx):
            x2 = (x + d) % nx
            last1[d] = send(sum1.at[p, pl.ds(pl.multiple_of(x2 * pr, pr), pr)], ry1.at[p, d], s2_s.at[p, 1, d], s2_r.at[p, 1, d], x2 * nz + z, c)
            last1[d].start()
        total0 = acc0[pl.ds(pl.multiple_of(z * pr, pr), pr), :]
        for d in order(nz):
            last0[d].wait_recv()
            total0 += ry0[p, d].astype(F32)
        total1 = acc1[pl.ds(pl.multiple_of(x * pr, pr), pr), :]
        for d in order(nx):
            last1[d].wait_recv()
            total1 += ry1[p, d].astype(F32)
        pending.extend(list(x_copies.values()) + list(z_copies.values()) + list(last0.values()) + list(last1.values()))
        return total0, total1

    eye = lax.broadcasted_iota(jnp.int32, (pr, pr), 0) == lax.broadcasted_iota(jnp.int32, (pr, pr), 1)
    den_col = jnp.sum(jnp.where(eye, jnp.broadcast_to(den[...], (pr, pr)), 0.0), axis=1, keepdims=True)

    totals = reduce_rows(0)
    for h in range(2):
        cols = slice(h * hv, (h + 1) * hv)
        sh = shifts[:, cols]
        start = vec[:, cols].astype(F32)
        resid = totals[h] - sh * start
        div = jnp.maximum(jnp.abs(den_col - sh), 1.0)
        nextv[:, cols] = (start - resid / div).astype(BF16)
    got1 = gather_start(1, nextv)
    gather_relay(1, got1)
    gather_end(1, got1)
    pending += list(got1.values())
    totals = reduce_rows(1)
    for h in range(2):
        prod_out[:, h * hv:(h + 1) * hv] = totals[h]
    next_out[...] = nextv[...]
    for cp in pending:
        cp.wait_send()


def local(nx, nz, ny, kernel, intersection, momentum, owner_pick, live_count, pair_slot, denominators, shifts, vectors):
    pr, nv = vectors.shape
    nq, cb, fb = intersection.shape
    nc = 2 * ny
    hv = nv // 2
    rows = nx * nz * pr
    wide = nc * pr
    hop = ny // 2
    dma = pltpu.SemaphoreType.DMA
    smem = pl.BlockSpec(memory_space=pltpu.SMEM)
    anyspace = pl.BlockSpec(memory_space=pl.ANY)
    vmem = pl.BlockSpec(memory_space=pltpu.VMEM)
    far = max(nx, nz)
    prod, nextv = pl.pallas_call(
        functools.partial(body, nx, nz, ny, fb),
        out_shape=(jax.ShapeDtypeStruct((pr, nv), F32), jax.ShapeDtypeStruct((pr, nv), BF16)),
        in_specs=[smem, smem, smem, smem, anyspace, anyspace, vmem, vmem, vmem],
        out_specs=(vmem, vmem),
        scratch_shapes=[
            pltpu.VMEM((nq, cb, fb), BF16),
            pltpu.VMEM((nc, 2, cb, cb), BF16),
            pltpu.VMEM((nc + 1, cb, wide), BF16),
            pltpu.VMEM((cb, wide), BF16),
            pltpu.VMEM((rows, wide), BF16),
            pltpu.VMEM((2, wide, nv), BF16),
            pltpu.VMEM((pr, nv), BF16),
            pltpu.VMEM((nc, 8, 128), jnp.int32),
            pltpu.VMEM((8, 128), jnp.int32),
            pltpu.VMEM((2, rows, hv), BF16),
            pltpu.VMEM((2, nz, nx * pr, hv), BF16),
            pltpu.VMEM((2, nx, nz * pr, hv), BF16),
            pltpu.VMEM((2, nz, nx * pr, hv), BF16),
            pltpu.VMEM((2, nz, pr, hv), BF16),
            pltpu.VMEM((2, nx, pr, hv), BF16),
            pltpu.VMEM((2, nz * pr, hv), BF16),
            pltpu.VMEM((2, nx * pr, hv), BF16),
            pltpu.VMEM((nz * pr, hv), F32),
            pltpu.VMEM((nx * pr, hv), F32),
            dma((2,)),
            dma((nc,)), dma((nc,)),
            dma((2, ny)), dma((2, ny)),
            dma((2, ny)), dma((2, ny)),
            dma((2, hop, 2)), dma((2, hop, 2)),
            dma((2, hop + 1, 2)), dma((2, hop + 1, 2)),
            dma((2, 2, far)), dma((2, 2, far)),
            dma((2, 2, far)), dma((2, 2, far)),
        ],
        compiler_params=pltpu.CompilerParams(collective_id=0, has_side_effects=True, vmem_limit_bytes=48 * 1024 * 1024),
    )(
        momentum, owner_pick, live_count, pair_slot, intersection, kernel,
        denominators.reshape(1, pr), shifts.reshape(1, nv), vectors,
    )
    next_float = nextv.astype(F32)
    divisor = jnp.maximum(jnp.abs(denominators[:, None] - shifts[None, :]), 1.0)
    residual = prod - shifts[None, :] * next_float
    return next_float - residual / divisor, residual


def build(mesh, nx, nz, ny):
    whole = P(("row", "col"))
    return jax.shard_map(
        functools.partial(local, nx, nz, ny),
        mesh=mesh,
        in_specs=(
            P(("row", "col"), None, None), P(), P(), whole, whole, P(("row", "col"), None), whole, P(), P(("row", "col"), None),
        ),
        out_specs=(P(("row", "col"), None), P(("row", "col"), None)),
        check_vma=False,
    )


def solution(mesh):
    return build(mesh, 8, 8, mesh.shape["col"] // 2)
```

```python
import functools

import jax
import jax.numpy as jnp
from jax import lax
from jax.experimental import pallas as pl
from jax.experimental.pallas import tpu as pltpu
from jax.sharding import PartitionSpec as P

F32 = jnp.float32
BF16 = jnp.bfloat16


def send(src, dst, send_sem, recv_sem, row, col):
    return pltpu.make_async_remote_copy(
        src_ref=src,
        dst_ref=dst,
        send_sem=send_sem,
        recv_sem=recv_sem,
        device_id={"row": row, "col": col},
        device_id_type=pl.DeviceIdType.MESH,
    )


def body(
    nx, nz, ny, fb,
    mom_hbm, picks_hbm, live_hbm, slots_hbm, inter_hbm, kern_hbm, den_hbm, shifts_hbm, vec_hbm,
    prod_out, next_out,
    mom, picks, live, slots, den, shifts, vec,
    inter, blk, half, basis, tile, held, heldn, nextv, pk, pk_own,
    part0, part1, near0, near1, pair0, pair1, rx0, rx1, ry0, ry1, sum0, sum1, acc0, acc1,
    loc, ag_s, ag_r, fw_s, fw_r, ring_s, ring_r, sib_s, sib_r, ringp_s, ringp_r, sibp_s, sibp_r,
    s0_s, s0_r, s1_s, s1_r, s2_s, s2_r,
):
    nc = 2 * ny
    pr, nv = vec.shape
    gv = nv // 2
    hr = pr // 2
    fc = nc * pr // fb
    chunk = nz * pr
    nblk = chunk // fb
    hop = ny // 2

    row = lax.axis_index("row")
    c = lax.axis_index("col")
    x, z = row // nz, row % nz
    y, core = c // 2, c % 2
    other = y * 2 + (1 - core)

    def bring(i, src, dst):
        cp = pltpu.make_async_copy(src, dst, loc.at[i])
        cp.start()
        return cp

    get_picks = bring(0, picks_hbm, picks)
    get_vec = bring(1, vec_hbm, vec)
    cb = kern_hbm.shape[1]
    own = []
    for k in range(2):
        own.append(bring(2 + 2 * k, kern_hbm.at[k], blk.at[c, k, pl.ds(0, cb)]))
        own.append(bring(3 + 2 * k, vec_hbm.at[pl.ds(k * hr, hr), pl.ds(0, cb)], blk.at[c, k, pl.ds(cb, hr)]))
    get_mom = bring(6, mom_hbm, mom)
    get_inter = bring(7, inter_hbm, inter)
    late = [bring(8, live_hbm, live), bring(9, slots_hbm, slots), bring(10, den_hbm, den), bring(11, shifts_hbm, shifts)]

    barrier = pltpu.get_barrier_semaphore()

    def greet(to_row, to_col):
        pl.semaphore_signal(barrier, inc=1, device_id={"row": to_row, "col": to_col}, device_id_type=pl.DeviceIdType.MESH)

    for d in range(1, nx):
        greet(((x + d) % nx) * nz + z, c)
    for d in range(1, nz):
        greet(x * nz + (z + d) % nz, c)
    for d in range(1, ny):
        greet(row, ((y + d) % ny) * 2 + core)
    greet(row, other)

    get_picks.wait()
    lane = lax.broadcasted_iota(jnp.int32, (8, 128), 1)
    mine = jnp.zeros((8, 128), jnp.int32)
    for j in range(nc):
        mine = jnp.where(lane == j, picks[j], mine)
    pk_own[...] = mine
    pk[c] = mine

    for cp in own:
        cp.wait()
    pl.semaphore_wait(barrier, nx - 1 + nz - 1 + ny - 1 + 1)

    pending = []

    def order(n):
        return [n // 2 + ((i + 1) // 2) * (1 - 2 * (i % 2)) for i in range(n - 1)]

    length = {(0, 0): hop, (0, 1): hop - 1, (1, 0): hop - 1, (1, 1): hop}
    lanes = [(0, 0), (1, 1), (0, 1), (1, 0)]
    step_to = [((y + 1) % ny) * 2 + core, ((y + ny - 1) % ny) * 2 + core]

    def source(way, t):
        return ((y - t) % ny if way == 0 else (y + t) % ny) * 2 + core

    def pass_on(way, t, k, src, to, sems):
        bs, br, ps, pq = sems
        out = [send(blk.at[src, k], blk.at[src, k], bs.at[way, t, k], br.at[way, t, k], row, to)]
        if k == 0:
            from_pk = pk_own if t == 0 else pk.at[src]
            out.append(send(from_pk.at[pl.ds(0, 1)], pk.at[src, pl.ds(0, 1)], ps.at[way, t], pq.at[way, t], row, to))
        for cp in out:
            cp.start()
        return out

    on_ring = (ring_s, ring_r, ringp_s, ringp_r)
    on_sib = (sib_s, sib_r, sibp_s, sibp_r)
    ring, sib = {}, {}
    for way, k in lanes:
        if length[way, k] >= 1:
            ring[way, 1, k] = pass_on(way, 0, k, c, step_to[way], on_ring)
    for k in range(2):
        sib[0, 0, k] = pass_on(0, 0, k, c, other, on_sib)

    get_mom.wait()
    get_inter.wait()
    get_vec.wait()
    for b in range(fc):
        basis[:, b * fb:(b + 1) * fb] = inter[mom[row * fc + b]]
    half[nc] = jnp.zeros(half.shape[1:], BF16)
    for cp in late:
        cp.wait()

    wide = fc * fb
    cut = min(wide, 2 * fb)

    def half_of(src):
        flag = jnp.sum(jnp.where(lax.broadcasted_iota(jnp.int32, (1, 128), 1) == c, pk[src][0:1, :], 0).astype(F32), axis=1, keepdims=True)
        for j in range(wide // cut):
            cols = slice(j * cut, (j + 1) * cut)
            second = jnp.broadcast_to(flag, (cb, cut)) > 0.5
            h0 = jnp.dot(blk[src, 0, 0:cb], basis[:, cols], preferred_element_type=F32)
            h1 = jnp.dot(blk[src, 1, 0:cb], basis[:, cols], preferred_element_type=F32)
            half[src, :, cols] = jnp.where(second, h1, h0).astype(BF16)
        for k in range(2):
            held[pl.ds(pl.multiple_of(src * pr + k * hr, hr), hr), :] = blk[src, k, cb:cb + hr]

    def halves(t):
        for way in range(1 if t == 0 else 2):
            for k in range(2):
                for cp in sib.get((way, t, k), []):
                    cp.wait_recv()
        if t == 0 or t == hop:
            spot = y if t == 0 else (y + hop) % ny

            def one(j, carry):
                half_of(spot * 2 + j)
                return carry

            lax.fori_loop(0, 2, one, 0)
        else:

            def one(j, carry):
                half_of(((y + ny + (1 - 2 * (j // 2)) * t) % ny) * 2 + j % 2)
                return carry

            lax.fori_loop(0, 4, one, 0)

    for t in range(1, hop + 1):
        for way, k in lanes:
            if t > length[way, k]:
                continue
            src = source(way, t)
            for cp in ring[way, t, k]:
                cp.wait_recv()
            if t < length[way, k]:
                ring[way, t + 1, k] = pass_on(way, t, k, src, step_to[way], on_ring)
            sib[way, t, k] = pass_on(way, t, k, src, other, on_sib)
        halves(t - 1)
    halves(hop)
    for many in list(ring.values()) + list(sib.values()):
        pending += many

    sense = 1 - 2 * core

    def pairs_of(n):
        pairs = [(s, s - 1) for s in range(n // 2, 1, -2)]
        pairs += [(-s, 1 - s) for s in range(n // 2 - 1, 1, -2)]
        taken = {s for pair in pairs for s in pair}
        return pairs, [s for s in [*range(1 - n // 2, 0), *range(1, n // 2 + 1)] if s not in taken]

    def dest(i, s, n):
        return (i + n - sense * s) % n

    def table(values, i, n):
        packed = sum((v % n) << (3 * j) for j, v in enumerate(values))
        return (jnp.int32(packed) >> (3 * i)) & 7

    def tile_rows(x2):
        return pl.ds(pl.multiple_of(x2 * chunk, chunk), chunk)

    def build_rows(x2):
        for q in range(nblk):
            a = x2 * nblk + q
            parts = []
            for b in range(fc):
                slot = slots[b, a]
                slot = jnp.where(slot < live[0], slot, nc)
                parts.append(half[slot, :, b * fb:(b + 1) * fb])
            picked = jnp.concatenate(parts, axis=1)
            u = inter[mom[c * (nx * nblk) + a]]
            fine = lax.dot_general(u, picked, (((0,), (0,)), ((), ())), preferred_element_type=F32)
            tile[pl.ds(pl.multiple_of(a * fb, fb), fb), :] = fine.astype(BF16)

    flight = {}

    def spread(p, g, build):
        def product(x2):
            if build:
                build_rows(x2)
            v = held[:, g * gv:(g + 1) * gv] if p == 0 else heldn[g]
            got = jnp.dot(tile[tile_rows(x2), :], v, preferred_element_type=F32).astype(BF16)
            for j in range(nz):
                part0[p, g, x2, j * hr:(j + 1) * hr, :] = got[j * pr:j * pr + hr]
                part1[p, g, j, pl.ds(pl.multiple_of(x2 * hr, hr), hr), :] = got[j * pr + hr:(j + 1) * pr]

        def far_copy(h, j, far, near):
            n, me = (nx, x) if h == 0 else (nz, z)
            to = (me + n + sense * (near - far)) % n
            part, into = (part0, near0) if h == 0 else (part1, near1)
            return send(part.at[p, g, dest(me, far, n)], into.at[p, g, j], s0_s.at[p, g, h, j], s0_r.at[p, g, h, j],
                        to * nz + z if h == 0 else x * nz + to, c)

        def step(i, carry):
            product(dest(x, table(order_of, i + start, nx), nx))
            return carry

        pairs, singles = pairs_of(nx)
        order_of = [far for far, near in pairs] + singles + [near for far, near in pairs] + [0]

        fars = {}
        start = 0
        for j, (far, near) in enumerate(pairs):
            fars[0, j] = far_copy(0, j, far, near)
        if pairs:

            def far_step(i, carry):
                far = table(order_of, i, nx)
                product(dest(x, far, nx))
                turn = table([(near - far) for far, near in pairs], i, nx)
                to = (x + nx + sense * turn) % nx
                send(part0.at[p, g, dest(x, far, nx)], near0.at[p, g, i], s0_s.at[p, g, 0, i], s0_r.at[p, g, 0, i], to * nz + z, c).start()
                return carry

            lax.fori_loop(0, len(pairs), far_step, 0)
        start = len(pairs)
        lax.fori_loop(0, nx - len(pairs), step, 0)
        direct = {}
        for h in range(2):
            n, me = (nx, x) if h == 0 else (nz, z)
            pairs, singles = pairs_of(n)
            if h == 1:
                for j, (far, near) in enumerate(pairs):
                    fars[1, j] = far_copy(1, j, far, near)
                    fars[1, j].start()
            part, rx = (part0, rx0) if h == 0 else (part1, rx1)
            for j, s in enumerate(singles):
                to = dest(me, s, n)
                cp = send(part.at[p, g, to], rx.at[p, g, len(pairs) + j], s1_s.at[p, g, h, len(pairs) + j], s1_r.at[p, g, h, len(pairs) + j],
                          to * nz + z if h == 0 else x * nz + to, c)
                cp.start()
                direct[h, len(pairs) + j] = cp
        flight[p, g] = [fars, direct]

    def relay(p, g):
        fars, direct = flight[p, g]
        for j in range(max(len(pairs_of(nx)[0]), len(pairs_of(nz)[0]))):
            for h in range(2):
                n, me = (nx, x) if h == 0 else (nz, z)
                pairs = pairs_of(n)[0]
                if j >= len(pairs):
                    continue
                to = dest(me, pairs[j][1], n)
                part, near, pair, rx = (part0, near0, pair0, rx0) if h == 0 else (part1, near1, pair1, rx1)
                fars[h, j].wait_recv()
                pair[p, g, j] = (part[p, g, to].astype(F32) + near[p, g, j].astype(F32)).astype(BF16)
                direct[h, j] = send(pair.at[p, g, j], rx.at[p, g, j], s1_s.at[p, g, h, j], s1_r.at[p, g, h, j],
                                    to * nz + z if h == 0 else x * nz + to, c)
                direct[h, j].start()

    def first_sums(p, g):
        direct = flight[p, g][1]
        last0, last1 = {}, {}
        for h in range(2):
            part, acc, rx, total = (part0, acc0, rx0, sum0) if h == 0 else (part1, acc1, rx1, sum1)
            sums = part[p, g, x if h == 0 else z].astype(F32)
            for j in sorted((j for way, j in direct if way == h), reverse=True):
                direct[h, j].wait_recv()
                sums += rx[p, g, j].astype(F32)
            acc[g] = sums
            total[p, g] = sums.astype(BF16)
            for d in order(nz if h == 0 else nx):
                to = (z + d) % nz if h == 0 else (x + d) % nx
                rows = pl.ds(pl.multiple_of(to * hr, hr), hr)
                if h == 0:
                    last0[d] = send(sum0.at[p, g, rows], ry0.at[p, g, d], s2_s.at[p, g, 0, d], s2_r.at[p, g, 0, d], x * nz + to, c)
                    last0[d].start()
                else:
                    last1[d] = send(sum1.at[p, g, rows], ry1.at[p, g, d], s2_s.at[p, g, 1, d], s2_r.at[p, g, 1, d], to * nz + z, c)
                    last1[d].start()
        flight[p, g] += [last0, last1]

    def last_sums(p, g):
        last0, last1 = flight[p, g][2:]
        total0 = acc0[g, pl.ds(pl.multiple_of(z * hr, hr), hr), :]
        for d, cp in last0.items():
            cp.wait_recv()
            total0 += ry0[p, g, d].astype(F32)
        total1 = acc1[g, pl.ds(pl.multiple_of(x * hr, hr), hr), :]
        for d, cp in last1.items():
            cp.wait_recv()
            total1 += ry1[p, g, d].astype(F32)
        for copies in flight[p, g]:
            pending.extend(copies.values())
        return jnp.concatenate([total0, total1], axis=0)

    mine_rows = pl.ds(pl.multiple_of(c * pr, pr), pr)

    def gather_start(g):
        copies = {}
        for d in order(ny):
            copies[d] = send(nextv.at[g], heldn.at[g, mine_rows], ag_s.at[g, d], ag_r.at[g, d], row, ((y + d) % ny) * 2 + core)
            copies[d].start()
        copies[0] = send(nextv.at[g], heldn.at[g, mine_rows], ag_s.at[g, 0], ag_r.at[g, 0], row, other)
        copies[0].start()
        return copies

    def gather_relay(g, copies):
        for d in sorted(range(1, ny), key=lambda d: min(d, ny - d)):
            copies[d].wait_recv()
            rows = pl.ds(pl.multiple_of((((y - d) % ny) * 2 + core) * pr, pr), pr)
            cp = send(heldn.at[g, rows], heldn.at[g, rows], fw_s.at[g, d], fw_r.at[g, d], row, other)
            cp.start()
            copies[ny + d] = cp

    def gather_end(g, copies):
        copies[0].wait_recv()
        for d in range(1, ny):
            copies[ny + d].wait_recv()
        pending.extend(copies.values())

    eye = lax.broadcasted_iota(jnp.int32, (pr, pr), 0) == lax.broadcasted_iota(jnp.int32, (pr, pr), 1)
    den_col = jnp.sum(jnp.where(eye, jnp.broadcast_to(den[...], (pr, pr)), 0.0), axis=1, keepdims=True)

    spread(0, 0, True)
    spread(0, 1, False)
    for g in range(2):
        relay(0, g)
    for g in range(2):
        first_sums(0, g)
    got = []
    for g in range(2):
        total = last_sums(0, g)
        cols = slice(g * gv, (g + 1) * gv)
        sh = shifts[:, cols]
        start = vec[:, cols].astype(F32)
        resid = total - sh * start
        div = jnp.maximum(jnp.abs(den_col - sh), 1.0)
        update = (start - resid / div).astype(BF16)
        nextv[g] = update
        heldn[g, mine_rows, :] = update
        next_out[:, cols] = update
        got.append(gather_start(g))
    for g in range(2):
        gather_relay(g, got[g])
    for g in range(2):
        gather_end(g, got[g])
        spread(1, g, False)
    for g in range(2):
        relay(1, g)
    for g in range(2):
        first_sums(1, g)
    for g in range(2):
        prod_out[:, g * gv:(g + 1) * gv] = last_sums(1, g)
    for cp in pending:
        cp.wait_send()


def local(nx, nz, ny, kernel, intersection, momentum, owner_pick, live_count, pair_slot, denominators, shifts, vectors):
    pr, nv = vectors.shape
    nq, cb, fb = intersection.shape
    nc = 2 * ny
    gv = nv // 2
    hr = pr // 2
    rows = nx * nz * pr
    wide = nc * pr
    fr, fc = pair_slot.shape
    hop = ny // 2
    dma = pltpu.SemaphoreType.DMA
    hbm = pl.BlockSpec(memory_space=pltpu.HBM)
    vmem = pl.BlockSpec(memory_space=pltpu.VMEM)
    far = max(nx, nz)
    few = max(1, far // 2 - 1)
    prod, nextv = pl.pallas_call(
        functools.partial(body, nx, nz, ny, fb),
        out_shape=(jax.ShapeDtypeStruct((pr, nv), F32), jax.ShapeDtypeStruct((pr, nv), BF16)),
        in_specs=[hbm] * 9,
        out_specs=(vmem, vmem),
        scratch_shapes=[
            pltpu.SMEM(momentum.shape, jnp.int32),
            pltpu.SMEM(owner_pick.shape, jnp.int32),
            pltpu.SMEM(live_count.shape, jnp.int32),
            pltpu.SMEM((fc, fr), jnp.int32),
            pltpu.VMEM((1, pr), F32),
            pltpu.VMEM((1, nv), F32),
            pltpu.VMEM((pr, nv), BF16),
            pltpu.VMEM((nq, cb, fb), BF16),
            pltpu.VMEM((nc, 2, cb + hr, cb), BF16),
            pltpu.VMEM((nc + 1, cb, wide), BF16),
            pltpu.VMEM((cb, wide), BF16),
            pltpu.VMEM((rows, wide), BF16),
            pltpu.VMEM((wide, nv), BF16),
            pltpu.VMEM((2, wide, gv), BF16),
            pltpu.VMEM((2, pr, gv), BF16),
            pltpu.VMEM((nc, 8, 128), jnp.int32),
            pltpu.VMEM((8, 128), jnp.int32),
            pltpu.VMEM((2, 2, nx, nz * hr, gv), BF16),
            pltpu.VMEM((2, 2, nz, nx * hr, gv), BF16),
            pltpu.VMEM((2, 2, few, nz * hr, gv), BF16),
            pltpu.VMEM((2, 2, few, nx * hr, gv), BF16),
            pltpu.VMEM((2, 2, few, nz * hr, gv), BF16),
            pltpu.VMEM((2, 2, few, nx * hr, gv), BF16),
            pltpu.VMEM((2, 2, few + 1, nz * hr, gv), BF16),
            pltpu.VMEM((2, 2, few + 1, nx * hr, gv), BF16),
            pltpu.VMEM((2, 2, nz, hr, gv), BF16),
            pltpu.VMEM((2, 2, nx, hr, gv), BF16),
            pltpu.VMEM((2, 2, nz * hr, gv), BF16),
            pltpu.VMEM((2, 2, nx * hr, gv), BF16),
            pltpu.VMEM((2, nz * hr, gv), F32),
            pltpu.VMEM((2, nx * hr, gv), F32),
            dma((12,)),
            dma((2, ny)), dma((2, ny)),
            dma((2, ny)), dma((2, ny)),
            dma((2, hop, 2)), dma((2, hop, 2)),
            dma((2, hop + 1, 2)), dma((2, hop + 1, 2)),
            dma((2, hop)), dma((2, hop)),
            dma((2, hop + 1)), dma((2, hop + 1)),
            dma((2, 2, 2, few)), dma((2, 2, 2, few)),
            dma((2, 2, 2, few + 1)), dma((2, 2, 2, few + 1)),
            dma((2, 2, 2, far)), dma((2, 2, 2, far)),
        ],
        compiler_params=pltpu.CompilerParams(collective_id=0, has_side_effects=True, vmem_limit_bytes=67_043_328),
    )(
        momentum, owner_pick, live_count, pair_slot.T, intersection, kernel,
        denominators.reshape(1, pr), shifts.reshape(1, nv), vectors,
    )
    next_float = nextv.astype(F32)
    divisor = jnp.maximum(jnp.abs(denominators[:, None] - shifts[None, :]), 1.0)
    residual = prod - shifts[None, :] * next_float
    return next_float - residual / divisor, residual


def build(mesh, nx, nz, ny):
    whole = P(("row", "col"))
    return jax.shard_map(
        functools.partial(local, nx, nz, ny),
        mesh=mesh,
        in_specs=(
            P(("row", "col"), None, None), P(), P(), whole, whole, P(("row", "col"), None), whole, P(), P(("row", "col"), None),
        ),
        out_specs=(P(("row", "col"), None), P(("row", "col"), None)),
        check_vma=False,
    )


def solution(mesh):
    return build(mesh, 8, 8, mesh.shape["col"] // 2)
```

```python
import functools

import jax
import jax.numpy as jnp
from jax import lax
from jax.experimental import pallas as pl
from jax.experimental.pallas import tpu as pltpu
from jax.sharding import PartitionSpec as P

F32 = jnp.float32
BF16 = jnp.bfloat16


def send(src, dst, send_sem, recv_sem, row, col):
    return pltpu.make_async_remote_copy(
        src_ref=src,
        dst_ref=dst,
        send_sem=send_sem,
        recv_sem=recv_sem,
        device_id={"row": row, "col": col},
        device_id_type=pl.DeviceIdType.MESH,
    )


def body(
    nx, nz, ny, fb,
    mom_hbm, picks_hbm, live_hbm, slots_hbm, inter_hbm, kern_hbm, den_hbm, shifts_hbm, vec_hbm,
    prod_out, next_out,
    mom, picks, live, slots, den, shifts, vec,
    inter, turned, blk, half, basis, tile, held, heldn, nextv, pk, pk_own,
    part0, part1, near0, near1, pair0, pair1, rx0, rx1, ry0, ry1, sum0, sum1, acc0, acc1,
    loc, ag_s, ag_r, fw_s, fw_r, ring_s, ring_r, sib_s, sib_r, ringp_s, ringp_r, sibp_s, sibp_r,
    s0_s, s0_r, s1_s, s1_r, s2_s, s2_r,
):
    nc = 2 * ny
    pr, nv = vec.shape
    gv = nv // 2
    hr = pr // 2
    fc = nc * pr // fb
    chunk = nz * pr
    nblk = chunk // fb
    hop = ny // 2

    row = lax.axis_index("row")
    c = lax.axis_index("col")
    x, z = row // nz, row % nz
    y, core = c // 2, c % 2
    other = y * 2 + (1 - core)

    def bring(i, src, dst):
        cp = pltpu.make_async_copy(src, dst, loc.at[i])
        cp.start()
        return cp

    get_picks = bring(0, picks_hbm, picks)
    get_vec = bring(1, vec_hbm, vec)
    cb = kern_hbm.shape[1]
    own = []
    for k in range(2):
        own.append(bring(2 + 2 * k, kern_hbm.at[k], blk.at[c, k, pl.ds(0, cb)]))
        own.append(bring(3 + 2 * k, vec_hbm.at[pl.ds(k * hr, hr), pl.ds(0, cb)], blk.at[c, k, pl.ds(cb, hr)]))
    get_mom = bring(6, mom_hbm, mom)
    get_inter = bring(7, inter_hbm, inter)
    late = [bring(8, live_hbm, live), bring(9, slots_hbm, slots), bring(10, den_hbm, den), bring(11, shifts_hbm, shifts)]

    barrier = pltpu.get_barrier_semaphore()

    def greet(to_row, to_col):
        pl.semaphore_signal(barrier, inc=1, device_id={"row": to_row, "col": to_col}, device_id_type=pl.DeviceIdType.MESH)

    for d in range(1, nx):
        greet(((x + d) % nx) * nz + z, c)
    for d in range(1, nz):
        greet(x * nz + (z + d) % nz, c)
    for d in range(1, ny):
        greet(row, ((y + d) % ny) * 2 + core)
    greet(row, other)

    get_picks.wait()
    lane = lax.broadcasted_iota(jnp.int32, (8, 128), 1)
    mine = jnp.zeros((8, 128), jnp.int32)
    for j in range(nc):
        mine = jnp.where(lane == j, picks[j], mine)
    pk_own[...] = mine
    pk[c] = mine

    for cp in own:
        cp.wait()
    pl.semaphore_wait(barrier, nx - 1 + nz - 1 + ny - 1 + 1)

    pending = []

    def order(n):
        return [n // 2 + ((i + 1) // 2) * (1 - 2 * (i % 2)) for i in range(n - 1)]

    length = {(0, 0): hop, (0, 1): hop - 1, (1, 0): hop - 1, (1, 1): hop}
    lanes = [(0, 0), (1, 1), (0, 1), (1, 0)]
    step_to = [((y + 1) % ny) * 2 + core, ((y + ny - 1) % ny) * 2 + core]

    def source(way, t):
        return ((y - t) % ny if way == 0 else (y + t) % ny) * 2 + core

    def pass_on(way, t, k, src, to, sems):
        bs, br, ps, pq = sems
        out = [send(blk.at[src, k], blk.at[src, k], bs.at[way, t, k], br.at[way, t, k], row, to)]
        if k == 0:
            from_pk = pk_own if t == 0 else pk.at[src]
            out.append(send(from_pk.at[pl.ds(0, 1)], pk.at[src, pl.ds(0, 1)], ps.at[way, t], pq.at[way, t], row, to))
        for cp in out:
            cp.start()
        return out

    on_ring = (ring_s, ring_r, ringp_s, ringp_r)
    on_sib = (sib_s, sib_r, sibp_s, sibp_r)
    ring, sib = {}, {}
    for way, k in lanes:
        if length[way, k] >= 1:
            ring[way, 1, k] = pass_on(way, 0, k, c, step_to[way], on_ring)
    for k in range(2):
        sib[0, 0, k] = pass_on(0, 0, k, c, other, on_sib)

    get_mom.wait()
    get_inter.wait()
    get_vec.wait()
    for b in range(fc):
        basis[:, b * fb:(b + 1) * fb] = inter[mom[row * fc + b]]
    half[nc] = jnp.zeros(half.shape[1:], BF16)
    for cp in late:
        cp.wait()

    wide = fc * fb
    cut = min(wide, 2 * fb)

    def half_of(src):
        flag = jnp.sum(jnp.where(lax.broadcasted_iota(jnp.int32, (1, 128), 1) == c, pk[src][0:1, :], 0).astype(F32), axis=1, keepdims=True)
        for j in range(wide // cut):
            cols = slice(j * cut, (j + 1) * cut)
            second = jnp.broadcast_to(flag, (cb, cut)) > 0.5
            h0 = jnp.dot(blk[src, 0, 0:cb], basis[:, cols], preferred_element_type=F32)
            h1 = jnp.dot(blk[src, 1, 0:cb], basis[:, cols], preferred_element_type=F32)
            half[src, :, cols] = jnp.where(second, h1, h0).astype(BF16)
        for k in range(2):
            held[pl.ds(pl.multiple_of(src * pr + k * hr, hr), hr), :] = blk[src, k, cb:cb + hr]

    def halves(t):
        if t == 0 or t == hop:
            half_of((y if t == 0 else (y + hop) % ny) * 2 + core)
        for way in range(1 if t == 0 else 2):
            for k in range(2):
                for cp in sib.get((way, t, k), []):
                    cp.wait_recv()
        if t == 0 or t == hop:
            half_of((y if t == 0 else (y + hop) % ny) * 2 + 1 - core)
        else:

            def one(j, carry):
                half_of(((y + ny + (1 - 2 * (j // 2)) * t) % ny) * 2 + j % 2)
                return carry

            lax.fori_loop(0, 4, one, 0)

    def turn_rows():
        def one(a, carry):
            turned[a] = inter[mom[c * (nx * nblk) + a]].T
            return carry

        lax.fori_loop(0, nx * nblk, one, 0)

    if hop == 0:
        turn_rows()
    for t in range(1, hop + 1):
        if t == hop:
            halves(t - 1)
        for way, k in lanes:
            if t > length[way, k]:
                continue
            src = source(way, t)
            for cp in ring[way, t, k]:
                cp.wait_recv()
            if t < length[way, k]:
                ring[way, t + 1, k] = pass_on(way, t, k, src, step_to[way], on_ring)
            sib[way, t, k] = pass_on(way, t, k, src, other, on_sib)
        if t < hop:
            halves(t - 1)
        if t == 1:
            turn_rows()
    halves(hop)
    for many in list(ring.values()) + list(sib.values()):
        pending += many

    sense = 1 - 2 * core

    def pairs_of(n):
        pairs = [(s, s - 1) for s in range(n // 2, 1, -2)]
        pairs += [(-s, 1 - s) for s in range(n // 2 - 1, 1, -2)]
        taken = {s for pair in pairs for s in pair}
        return pairs, [s for s in [*range(1 - n // 2, 0), *range(1, n // 2 + 1)] if s not in taken]

    def dest(i, s, n):
        return (i + n - sense * s) % n

    def table(values, i, n):
        packed = sum((v % n) << (3 * j) for j, v in enumerate(values))
        return (jnp.int32(packed) >> (3 * i)) & 7

    def tile_rows(x2):
        return pl.ds(pl.multiple_of(x2 * chunk, chunk), chunk)

    def build_rows(x2):
        for q in range(nblk):
            a = x2 * nblk + q
            parts = []
            for b in range(fc):
                slot = slots[b, a]
                slot = jnp.where(slot < live[0], slot, nc)
                parts.append(half[slot, :, b * fb:(b + 1) * fb])
            picked = jnp.concatenate(parts, axis=1)
            fine = jnp.dot(turned[a], picked, preferred_element_type=F32)
            tile[pl.ds(pl.multiple_of(a * fb, fb), fb), :] = fine.astype(BF16)

    flight = {}

    def spread(p, g, build):
        def product(x2):
            if p == 0 and not build:
                return
            if build:
                build_rows(x2)
            v = held[...] if build else heldn[g]
            got = jnp.dot(tile[tile_rows(x2), :], v, preferred_element_type=F32).astype(BF16)
            for w in (0, 1) if build else (g,):
                cols = slice(w * gv, (w + 1) * gv) if build else slice(0, gv)
                for j in range(nz):
                    part0[p, w, x2, j * hr:(j + 1) * hr, :] = got[j * pr:j * pr + hr, cols]
                    part1[p, w, j, pl.ds(pl.multiple_of(x2 * hr, hr), hr), :] = got[j * pr + hr:(j + 1) * pr, cols]

        def far_copy(h, j, far, near):
            n, me = (nx, x) if h == 0 else (nz, z)
            to = (me + n + sense * (near - far)) % n
            part, into = (part0, near0) if h == 0 else (part1, near1)
            return send(part.at[p, g, dest(me, far, n)], into.at[p, g, j], s0_s.at[p, g, h, j], s0_r.at[p, g, h, j],
                        to * nz + z if h == 0 else x * nz + to, c)

        def step(i, carry):
            product(dest(x, table(order_of, i + start, nx), nx))
            return carry

        pairs, singles = pairs_of(nx)
        order_of = [far for far, near in pairs] + singles + [near for far, near in pairs] + [0]

        fars = {}
        start = 0
        for j, (far, near) in enumerate(pairs):
            fars[0, j] = far_copy(0, j, far, near)
        if pairs:

            def far_step(i, carry):
                far = table(order_of, i, nx)
                product(dest(x, far, nx))
                turn = table([(near - far) for far, near in pairs], i, nx)
                to = (x + nx + sense * turn) % nx
                send(part0.at[p, g, dest(x, far, nx)], near0.at[p, g, i], s0_s.at[p, g, 0, i], s0_r.at[p, g, 0, i], to * nz + z, c).start()
                return carry

            lax.fori_loop(0, len(pairs), far_step, 0)
        start = len(pairs)
        if p == 1 or build:
            lax.fori_loop(0, nx - len(pairs), step, 0)
        direct = {}
        for h in range(2):
            n, me = (nx, x) if h == 0 else (nz, z)
            pairs, singles = pairs_of(n)
            if h == 1:
                for j, (far, near) in enumerate(pairs):
                    fars[1, j] = far_copy(1, j, far, near)
                    fars[1, j].start()
            part, rx = (part0, rx0) if h == 0 else (part1, rx1)
            for j, s in enumerate(singles):
                to = dest(me, s, n)
                cp = send(part.at[p, g, to], rx.at[p, g, len(pairs) + j], s1_s.at[p, g, h, len(pairs) + j], s1_r.at[p, g, h, len(pairs) + j],
                          to * nz + z if h == 0 else x * nz + to, c)
                cp.start()
                direct[h, len(pairs) + j] = cp
        flight[p, g] = [fars, direct]

    def relay(p, g):
        fars, direct = flight[p, g]
        for j in range(max(len(pairs_of(nx)[0]), len(pairs_of(nz)[0]))):
            for h in range(2):
                n, me = (nx, x) if h == 0 else (nz, z)
                pairs = pairs_of(n)[0]
                if j >= len(pairs):
                    continue
                to = dest(me, pairs[j][1], n)
                part, near, pair, rx = (part0, near0, pair0, rx0) if h == 0 else (part1, near1, pair1, rx1)
                fars[h, j].wait_recv()
                pair[p, g, j] = (part[p, g, to].astype(F32) + near[p, g, j].astype(F32)).astype(BF16)
                direct[h, j] = send(pair.at[p, g, j], rx.at[p, g, j], s1_s.at[p, g, h, j], s1_r.at[p, g, h, j],
                                    to * nz + z if h == 0 else x * nz + to, c)
                direct[h, j].start()

    def first_sums(p, g):
        direct = flight[p, g][1]
        last0, last1 = {}, {}
        for h in range(2):
            part, acc, rx, total = (part0, acc0, rx0, sum0) if h == 0 else (part1, acc1, rx1, sum1)
            sums = part[p, g, x if h == 0 else z].astype(F32)
            for j in sorted((j for way, j in direct if way == h), reverse=True):
                direct[h, j].wait_recv()
                sums += rx[p, g, j].astype(F32)
            acc[g] = sums
            total[p, g] = sums.astype(BF16)
            for d in order(nz if h == 0 else nx):
                to = (z + d) % nz if h == 0 else (x + d) % nx
                rows = pl.ds(pl.multiple_of(to * hr, hr), hr)
                if h == 0:
                    last0[d] = send(sum0.at[p, g, rows], ry0.at[p, g, d], s2_s.at[p, g, 0, d], s2_r.at[p, g, 0, d], x * nz + to, c)
                    last0[d].start()
                else:
                    last1[d] = send(sum1.at[p, g, rows], ry1.at[p, g, d], s2_s.at[p, g, 1, d], s2_r.at[p, g, 1, d], to * nz + z, c)
                    last1[d].start()
        flight[p, g] += [last0, last1]

    def last_sums(p, g):
        last0, last1 = flight[p, g][2:]
        total0 = acc0[g, pl.ds(pl.multiple_of(z * hr, hr), hr), :]
        for d, cp in last0.items():
            cp.wait_recv()
            total0 += ry0[p, g, d].astype(F32)
        total1 = acc1[g, pl.ds(pl.multiple_of(x * hr, hr), hr), :]
        for d, cp in last1.items():
            cp.wait_recv()
            total1 += ry1[p, g, d].astype(F32)
        for copies in flight[p, g]:
            pending.extend(copies.values())
        return jnp.concatenate([total0, total1], axis=0)

    mine_rows = pl.ds(pl.multiple_of(c * pr, pr), pr)

    def gather_start(g):
        copies = {}
        for d in order(ny):
            copies[d] = send(nextv.at[g], heldn.at[g, mine_rows], ag_s.at[g, d], ag_r.at[g, d], row, ((y + d) % ny) * 2 + core)
            copies[d].start()
        copies[0] = send(nextv.at[g], heldn.at[g, mine_rows], ag_s.at[g, 0], ag_r.at[g, 0], row, other)
        copies[0].start()
        return copies

    def gather_relay(g, copies):
        for d in sorted(range(1, ny), key=lambda d: min(d, ny - d)):
            copies[d].wait_recv()
            rows = pl.ds(pl.multiple_of((((y - d) % ny) * 2 + core) * pr, pr), pr)
            cp = send(heldn.at[g, rows], heldn.at[g, rows], fw_s.at[g, d], fw_r.at[g, d], row, other)
            cp.start()
            copies[ny + d] = cp

    def gather_end(g, copies):
        copies[0].wait_recv()
        for d in range(1, ny):
            copies[ny + d].wait_recv()
        pending.extend(copies.values())

    eye = lax.broadcasted_iota(jnp.int32, (pr, pr), 0) == lax.broadcasted_iota(jnp.int32, (pr, pr), 1)
    den_col = jnp.sum(jnp.where(eye, jnp.broadcast_to(den[...], (pr, pr)), 0.0), axis=1, keepdims=True)

    spread(0, 0, True)
    spread(0, 1, False)
    for g in range(2):
        relay(0, g)
    for g in range(2):
        first_sums(0, g)
    got = []
    for g in range(2):
        total = last_sums(0, g)
        cols = slice(g * gv, (g + 1) * gv)
        sh = shifts[:, cols]
        start = vec[:, cols].astype(F32)
        resid = total - sh * start
        div = jnp.maximum(jnp.abs(den_col - sh), 1.0)
        update = (start - resid / div).astype(BF16)
        nextv[g] = update
        heldn[g, mine_rows, :] = update
        next_out[:, cols] = update
        got.append(gather_start(g))
    for g in range(2):
        gather_relay(g, got[g])
    for g in range(2):
        gather_end(g, got[g])
        spread(1, g, False)
    for g in range(2):
        relay(1, g)
    for g in range(2):
        first_sums(1, g)
    for g in range(2):
        prod_out[:, g * gv:(g + 1) * gv] = last_sums(1, g)
    for cp in pending:
        cp.wait_send()


def local(nx, nz, ny, kernel, intersection, momentum, owner_pick, live_count, pair_slot, denominators, shifts, vectors):
    pr, nv = vectors.shape
    nq, cb, fb = intersection.shape
    nc = 2 * ny
    gv = nv // 2
    hr = pr // 2
    rows = nx * nz * pr
    wide = nc * pr
    fr, fc = pair_slot.shape
    hop = ny // 2
    dma = pltpu.SemaphoreType.DMA
    hbm = pl.BlockSpec(memory_space=pltpu.HBM)
    vmem = pl.BlockSpec(memory_space=pltpu.VMEM)
    far = max(nx, nz)
    few = max(1, far // 2 - 1)
    prod, nextv = pl.pallas_call(
        functools.partial(body, nx, nz, ny, fb),
        out_shape=(jax.ShapeDtypeStruct((pr, nv), F32), jax.ShapeDtypeStruct((pr, nv), BF16)),
        in_specs=[hbm] * 9,
        out_specs=(vmem, vmem),
        scratch_shapes=[
            pltpu.SMEM(momentum.shape, jnp.int32),
            pltpu.SMEM(owner_pick.shape, jnp.int32),
            pltpu.SMEM(live_count.shape, jnp.int32),
            pltpu.SMEM((fc, fr), jnp.int32),
            pltpu.VMEM((1, pr), F32),
            pltpu.VMEM((1, nv), F32),
            pltpu.VMEM((pr, nv), BF16),
            pltpu.VMEM((nq, cb, fb), BF16),
            pltpu.VMEM((fr, fb, cb), BF16),
            pltpu.VMEM((nc, 2, cb + hr, cb), BF16),
            pltpu.VMEM((nc + 1, cb, wide), BF16),
            pltpu.VMEM((cb, wide), BF16),
            pltpu.VMEM((rows, wide), BF16),
            pltpu.VMEM((wide, nv), BF16),
            pltpu.VMEM((2, wide, gv), BF16),
            pltpu.VMEM((2, pr, gv), BF16),
            pltpu.VMEM((nc, 8, 128), jnp.int32),
            pltpu.VMEM((8, 128), jnp.int32),
            pltpu.VMEM((2, 2, nx, nz * hr, gv), BF16),
            pltpu.VMEM((2, 2, nz, nx * hr, gv), BF16),
            pltpu.VMEM((2, 2, few, nz * hr, gv), BF16),
            pltpu.VMEM((2, 2, few, nx * hr, gv), BF16),
            pltpu.VMEM((2, 2, few, nz * hr, gv), BF16),
            pltpu.VMEM((2, 2, few, nx * hr, gv), BF16),
            pltpu.VMEM((2, 2, few + 1, nz * hr, gv), BF16),
            pltpu.VMEM((2, 2, few + 1, nx * hr, gv), BF16),
            pltpu.VMEM((2, 2, nz, hr, gv), BF16),
            pltpu.VMEM((2, 2, nx, hr, gv), BF16),
            pltpu.VMEM((2, 2, nz * hr, gv), BF16),
            pltpu.VMEM((2, 2, nx * hr, gv), BF16),
            pltpu.VMEM((2, nz * hr, gv), F32),
            pltpu.VMEM((2, nx * hr, gv), F32),
            dma((12,)),
            dma((2, ny)), dma((2, ny)),
            dma((2, ny)), dma((2, ny)),
            dma((2, hop, 2)), dma((2, hop, 2)),
            dma((2, hop + 1, 2)), dma((2, hop + 1, 2)),
            dma((2, hop)), dma((2, hop)),
            dma((2, hop + 1)), dma((2, hop + 1)),
            dma((2, 2, 2, few)), dma((2, 2, 2, few)),
            dma((2, 2, 2, few + 1)), dma((2, 2, 2, few + 1)),
            dma((2, 2, 2, far)), dma((2, 2, 2, far)),
        ],
        compiler_params=pltpu.CompilerParams(collective_id=0, has_side_effects=True, vmem_limit_bytes=67_043_328),
    )(
        momentum, owner_pick, live_count, pair_slot.T, intersection, kernel,
        denominators.reshape(1, pr), shifts.reshape(1, nv), vectors,
    )
    next_float = nextv.astype(F32)
    divisor = jnp.maximum(jnp.abs(denominators[:, None] - shifts[None, :]), 1.0)
    residual = prod - shifts[None, :] * next_float
    return next_float - residual / divisor, residual


def build(mesh, nx, nz, ny):
    whole = P(("row", "col"))
    return jax.shard_map(
        functools.partial(local, nx, nz, ny),
        mesh=mesh,
        in_specs=(
            P(("row", "col"), None, None), P(), P(), whole, whole, P(("row", "col"), None), whole, P(), P(("row", "col"), None),
        ),
        out_specs=(P(("row", "col"), None), P(("row", "col"), None)),
        check_vma=False,
    )


def solution(mesh):
    return build(mesh, 8, 8, mesh.shape["col"] // 2)
```
